32 devices in a mesh: row: 4 (over x, core), col: 8 (over z, y).
Axes of the slice: x: 2, y: 2, z: 4, core: 2. Of those that a mesh axis runs over, the one named last changes fastest.
Arguments:
- left_factor: bfloat16 [128, 32, 2048], P('col', None, 'row'), may hold values from -6 to 6
- right_factor: bfloat16 [128, 32, 2048], P('row', None, 'col'), may hold values from -6 to 6
- pair_grad: bfloat16 [2048, 128, 2048], P('row', None, 'col'), may hold values from -6 to 6
- projection: bfloat16 [1024, 128], replicated, may hold values from -0.1875 to 0.1875
Outputs:
- left_grad: float32 [128, 32, 2048], P('col', None, 'row')
- right_grad: float32 [128, 32, 2048], P('row', None, 'col')
The draws below stay inside these ranges and needn't reach their ends.
All inputs are finite; a program needn't handle non-finite values.
Results may differ from the reference program's by a relative error of at most 0.0029.
Values may be sent and summed in bfloat16 or wider, within the bound.
A program may use at most 576 MiB of HBM per device.

```python
import jax
import jax.numpy as jnp
from jax import lax

C = 32
CZ = 128
NRES = 2048
SEQS = 128


def level_of(key, extent, split, least, high):
    def one(position, shards_of):
        steps = jax.random.uniform(jax.random.fold_in(jax.random.fold_in(key, 6), position), (shards_of,), jnp.float32, least / len(split), high / len(split))
        return jnp.repeat(jnp.exp(steps), extent[position] // shards_of).reshape((-1,) + (1,) * (len(extent) - position - 1))

    level = one(*split[0])
    for cut in split[1:]:
        level = level * one(*cut)
    return level


def normal_values(stream_key, extent, deviation, bound, shards=(), dtype=jnp.bfloat16):
    loudness = level_of(stream_key, extent, shards, -0.22, 0.18) if shards else 1.0
    drawn = jax.random.normal(stream_key, extent, jnp.float32) * deviation * loudness
    return jnp.minimum(jnp.maximum(drawn, -bound), bound).astype(dtype)


def setup_inputs(seed: int = 0) -> dict:
    key_of = jax.random.split(jax.random.key(seed), 5)
    left_factor = normal_values(key_of[0], (SEQS, C, NRES), 1.0, 6.0, ((0, 8), (2, 4)))
    right_factor = normal_values(key_of[1], (SEQS, C, NRES), 1.0, 6.0, ((0, 4), (2, 8)))
    pair_grad = normal_values(key_of[2], (NRES, CZ, NRES), 1.0, 6.0, ((0, 4), (2, 8)))
    projection = normal_values(key_of[3], (C * C, CZ), (C * C) ** -0.5, 0.1875)
    return {"left_factor": left_factor, "right_factor": right_factor, "pair_grad": pair_grad, "projection": projection}


def reference(left_factor, right_factor, pair_grad, projection):
    total = pair_grad.shape[0]
    height = 32
    counted = total // height
    inverse = 1.0 / SEQS
    left_wide = left_factor.astype(jnp.float32)
    right_wide = right_factor.astype(jnp.float32)

    def advance(right_sum, offset):
        slab = lax.dynamic_slice_in_dim(pair_grad, offset, height, 0)
        slab = jnp.moveaxis(slab, 1, 2)
        expanded = jnp.dot(slab.reshape(height * total, CZ), projection.T, preferred_element_type=jnp.float32)
        expanded = expanded.astype(jnp.bfloat16).astype(jnp.float32).reshape(height, total, C, C)
        left_piece = jnp.einsum("ijce,sej->sci", expanded, right_wide) * inverse
        left_slab = lax.dynamic_slice_in_dim(left_wide, offset, height, 2)
        right_sum = right_sum + jnp.einsum("ijce,sci->sej", expanded, left_slab)
        return right_sum, left_piece

    offsets = (jnp.arange(counted) * height).astype(jnp.int32)
    right_sum, left_pieces = lax.scan(advance, jnp.zeros((SEQS, C, total), jnp.float32), offsets)
    left_grad = jnp.moveaxis(left_pieces, 0, 2).reshape(SEQS, C, total)
    right_grad = right_sum * inverse
    return left_grad, right_grad
```

```python
import functools

import jax
import jax.numpy as jnp
from jax import lax
from jax.experimental import pallas as pl
from jax.experimental.pallas import tpu as pltpu
from jax.sharding import PartitionSpec as P

CHUNKS = 4
BLOCK_ROWS = 16
PASSES = 2
FUSED_ROWS = 32
UNITS = 4
MESH = pl.DeviceIdType.MESH
BF16 = jnp.bfloat16
F32 = jnp.float32


def fused_block(
    n_row, n_col, channels, proj_ref, grad_ref, left_ref, right_ref, out_left_ref, out_right_ref,
    held_0, held_1, grads, lefts, rights, right_sum, left_sum, left_out, left_in, right_out, right_in, left_done,
    right_done, grad_sem, own_sem, left_send, left_recv, right_send, right_recv, part_send, part_recv, sum_send, sum_recv,
):
    tile_rows, width, cols = grad_ref.shape
    own, right_own = left_ref.shape[0], right_ref.shape[0]
    sequences = own * n_col
    inverse = 1.0 / sequences
    rows = FUSED_ROWS
    blocks = tile_rows // rows
    chunks = blocks // 2
    pairs = PASSES * chunks
    some = channels // PASSES
    high = some * channels
    wide = some * cols
    deep = rows * channels
    span = 2 * deep
    per_unit = rows // UNITS
    step = wide // UNITS
    row, col = lax.axis_index("row"), lax.axis_index("col")

    def to_col(d):
        return {"col": lax.rem(col + d, n_col)}

    def to_row(d):
        return {"row": lax.rem(row + d, n_row)}

    def left_copy(d, k):
        at = pl.ds(pl.multiple_of(k * span, span), span)
        return pltpu.make_async_remote_copy(
            left_ref.at[:, at], lefts.at[pl.ds(pl.multiple_of(col * own, own), own), at],
            left_send.at[d - 1, k], left_recv.at[d - 1, k], device_id=to_col(d), device_id_type=MESH,
        )

    def right_copy(d, h):
        at = pl.ds(pl.multiple_of(h * wide, wide), wide)
        return pltpu.make_async_remote_copy(
            right_ref.at[:, at], rights.at[pl.ds(pl.multiple_of(row * right_own, right_own), right_own), at],
            right_send.at[d - 1, h], right_recv.at[d - 1, h], device_id=to_row(d), device_id_type=MESH,
        )

    def part_copy(d, k):
        at = pl.ds(pl.multiple_of(k * span, span), span)
        to = lax.rem(col + d, n_col)
        return pltpu.make_async_remote_copy(
            left_out.at[pl.ds(pl.multiple_of(to * own, own), own), at], left_in.at[d - 1, :, at],
            part_send.at[d - 1, k], part_recv.at[d - 1, k], device_id=to_col(d), device_id_type=MESH,
        )

    def sum_copy(d, h):
        at = pl.ds(pl.multiple_of(h * wide, wide), wide)
        to = lax.rem(row + d, n_row)
        return pltpu.make_async_remote_copy(
            right_out.at[pl.ds(pl.multiple_of(to * right_own, right_own), right_own), at], right_in.at[d - 1, :, at],
            sum_send.at[d - 1, h], sum_recv.at[d - 1, h], device_id=to_row(d), device_id_type=MESH,
        )

    def grad_copy(t, slot):
        at = lax.rem(t, blocks) * rows
        return pltpu.make_async_copy(grad_ref.at[pl.ds(at, rows)], grads.at[slot], grad_sem.at[slot])

    own_left = pltpu.make_async_copy(left_ref, lefts.at[pl.ds(pl.multiple_of(col * own, own), own)], own_sem.at[0])
    own_right = pltpu.make_async_copy(right_ref, rights.at[pl.ds(pl.multiple_of(row * right_own, right_own), right_own)], own_sem.at[1])

    barrier = pltpu.get_barrier_semaphore()

    @pl.loop(1, n_col)
    def _(d):
        pl.semaphore_signal(barrier, inc=1, device_id=to_col(d), device_id_type=MESH)

    @pl.loop(1, n_row)
    def _(d):
        pl.semaphore_signal(barrier, inc=1, device_id=to_row(d), device_id_type=MESH)

    grad_copy(0, 0).start()
    grad_copy(1, 1).start()
    own_left.start()
    own_right.start()
    pl.semaphore_wait(barrier, n_col + n_row - 2)

    @pl.loop(0, PASSES)
    def _(h):
        @pl.loop(1, n_row)
        def _(d):
            right_copy(d, h).start()

    @pl.loop(0, chunks)
    def _(k):
        @pl.loop(1, n_col)
        def _(d):
            left_copy(d, k).start()

    right_sum[...] = jnp.zeros_like(right_sum)
    left_sum[...] = jnp.zeros_like(left_sum)

    def produce(n, h, slot, held):
        rows_of = pl.ds(pl.multiple_of(h * high, high), high)
        for r in range(per_unit):
            i = n * per_unit + r
            out = jnp.dot(proj_ref[rows_of, :], grads[slot, i], preferred_element_type=F32).astype(BF16)
            at = pl.ds(pl.multiple_of(i * channels, channels), channels)
            for e in range(some):
                held[at, e * cols : (e + 1) * cols] = out[e * channels : (e + 1) * channels]

    def consume(n, h, b, held):
        inside = pl.ds(pl.multiple_of(n * step, step), step)
        outside = pl.ds(pl.multiple_of(h * wide + n * step, step), step)
        deep_at = pl.ds(pl.multiple_of(b * deep, deep), deep)
        part = held[:, inside]
        right_sum[:, outside] += jnp.dot(lefts[:, deep_at], part, preferred_element_type=F32)
        left_sum[deep_at, :] += lax.dot_general(
            part, rights[:, outside], (((1,), (1,)), ((), ())), preferred_element_type=F32
        )

    def finish_left(k):
        piece = min(512, span)

        @pl.loop(0, span // piece)
        def _(q):
            at = pl.ds(pl.multiple_of(k * span + q * piece, piece), piece)
            left_out[:, at] = left_sum[at, :].astype(BF16).T

        return None

    def finish_right(h):
        piece = min(512, wide)

        @pl.loop(0, wide // piece)
        def _(q):
            at = pl.ds(pl.multiple_of(h * wide + q * piece, piece), piece)
            right_out[:, at] = right_sum[:, at].astype(BF16)

        return None

    def send_left(k):
        @pl.loop(1, n_col)
        def _(d):
            part_copy(d, k).start()

    def send_right(h):
        @pl.loop(1, n_row)
        def _(d):
            sum_copy(d, h).start()

    def total_left(k):
        @pl.loop(1, n_col)
        def _(d):
            part_copy(d, k).wait_recv()

        piece = min(512, span)

        @pl.loop(0, span // piece)
        def _(q):
            at = pl.ds(pl.multiple_of(k * span + q * piece, piece), piece)
            total = left_out[pl.ds(pl.multiple_of(col * own, own), own), at].astype(F32)
            for d in range(n_col - 1):
                total += left_in[d, :, at].astype(F32)
            left_done[:, at] = total * inverse

    def total_right(h):
        @pl.loop(1, n_row)
        def _(d):
            sum_copy(d, h).wait_recv()

        piece = min(512, wide)

        @pl.loop(0, wide // piece)
        def _(q):
            at = pl.ds(pl.multiple_of(h * wide + q * piece, piece), piece)
            total = right_sum[pl.ds(pl.multiple_of(row * right_own, right_own), right_own), at]
            for d in range(n_row - 1):
                total += right_in[d, :, at].astype(F32)
            right_done[:, at] = total * inverse

    def wait_right(h):
        @pl.loop(1, n_row)
        def _(d):
            right_copy(d, h).wait_recv()

    grad_copy(0, 0).wait()

    @pl.loop(0, UNITS)
    def _(n):
        produce(n, 0, 0, held_0)

    own_left.wait()
    own_right.wait()
    wait_right(0)

    def first_half(p):
        h, b = p // chunks, lax.rem(p, chunks) * 2

        @pl.when(p < chunks)
        def _():
            @pl.loop(1, n_col)
            def _(d):
                left_copy(d, p).wait_recv()

        @pl.when(p == chunks)
        def _():
            wait_right(1)

        grad_copy(2 * p + 1, 1).wait()

        @pl.when(p < pairs - 1)
        def _():
            grad_copy(2 * p + 2, 0).start()

        @pl.loop(0, UNITS)
        def _(n):
            produce(n, h, 1, held_1)
            consume(n, h, b, held_0)

        @pl.when(p == chunks)
        def _():
            send_right(0)

        @pl.when(p > chunks)
        def _():
            send_left(p - chunks - 1)

    @pl.loop(0, pairs - 1)
    def _(p):
        first_half(p)
        h, b = p // chunks, lax.rem(p, chunks) * 2 + 1
        ahead = (p + 1) // chunks
        grad_copy(2 * p + 2, 0).wait()
        grad_copy(2 * p + 3, 1).start()

        @pl.loop(0, UNITS)
        def _(n):
            produce(n, ahead, 0, held_0)
            consume(n, h, b, held_1)

        @pl.when(p == chunks - 1)
        def _():
            finish_right(0)

        @pl.when(p >= chunks)
        def _():
            finish_left(p - chunks)

    first_half(pairs - 1)

    @pl.loop(0, UNITS)
    def _(n):
        consume(n, PASSES - 1, blocks - 1, held_1)

    finish_right(1)
    finish_left(chunks - 1)
    send_right(1)
    send_left(chunks - 1)

    total_right(0)

    @pl.loop(0, chunks - 1)
    def _(k):
        total_left(k)

    total_left(chunks - 1)
    left_copy_out = pltpu.make_async_copy(left_done, out_left_ref, own_sem.at[0])
    left_copy_out.start()
    total_right(1)
    right_copy_out = pltpu.make_async_copy(right_done, out_right_ref, own_sem.at[1])
    right_copy_out.start()

    @pl.loop(0, chunks)
    def _(k):
        @pl.loop(1, n_col)
        def _(d):
            left_copy(d, k).wait_send()
            part_copy(d, k).wait_send()

    @pl.loop(0, PASSES)
    def _(h):
        @pl.loop(1, n_row)
        def _(d):
            right_copy(d, h).wait_send()
            sum_copy(d, h).wait_send()

    left_copy_out.wait()
    right_copy_out.wait()


def fused(proj, grad, left, right, n_row, n_col):
    tile_rows, width, cols = grad.shape
    own, right_own = left.shape[0], right.shape[0]
    channels = left.shape[1] // tile_rows
    sequences = own * n_col
    rows = FUSED_ROWS
    chunks = tile_rows // rows // 2
    flops = 2 * tile_rows * cols * channels * channels * (width + 2 * sequences)
    anywhere = pl.BlockSpec(memory_space=pl.ANY)
    held = pltpu.VMEM((rows * channels, channels // PASSES * cols), BF16)
    dma = pltpu.SemaphoreType.DMA
    return pl.pallas_call(
        functools.partial(fused_block, n_row, n_col, channels),
        in_specs=[pl.BlockSpec(memory_space=pltpu.VMEM), anywhere, anywhere, anywhere],
        out_specs=[anywhere, anywhere],
        out_shape=[jax.ShapeDtypeStruct(left.shape, F32), jax.ShapeDtypeStruct(right.shape, F32)],
        scratch_shapes=[
            held,
            held,
            pltpu.VMEM((2, rows, width, cols), BF16),
            pltpu.VMEM((sequences, tile_rows * channels), BF16),
            pltpu.VMEM((sequences, channels * cols), BF16),
            pltpu.VMEM((sequences, channels * cols), F32),
            pltpu.VMEM((tile_rows * channels, sequences), F32),
            pltpu.VMEM((sequences, tile_rows * channels), BF16),
            pltpu.VMEM((n_col - 1, own, tile_rows * channels), BF16),
            pltpu.VMEM((sequences, channels * cols), BF16),
            pltpu.VMEM((n_row - 1, right_own, channels * cols), BF16),
            pltpu.VMEM(left.shape, F32),
            pltpu.VMEM(right.shape, F32),
            dma((2,)),
            dma((2,)),
            dma((n_col - 1, chunks)),
            dma((n_col - 1, chunks)),
            dma((n_row - 1, PASSES)),
            dma((n_row - 1, PASSES)),
            dma((n_col - 1, chunks)),
            dma((n_col - 1, chunks)),
            dma((n_row - 1, PASSES)),
            dma((n_row - 1, PASSES)),
        ],
        compiler_params=pltpu.CompilerParams(
            collective_id=0, has_side_effects=True, vmem_limit_bytes=62 * 1024 * 1024
        ),
        cost_estimate=pl.CostEstimate(flops=flops, bytes_accessed=2 * grad.size * 2, transcendentals=0),
    )(proj, grad, left, right)


def contract_block(channels, cols, inverse, proj_ref, grad_ref, left_ref, right_ref, before_ref, out_left_ref, sum_ref, held):
    rows = grad_ref.shape[0]

    @pl.when(pl.program_id(0) == 0)
    def _():
        sum_ref[...] = before_ref[...]

    @pl.loop(0, rows)
    def _(i):
        wide = jnp.dot(proj_ref[...], grad_ref[i], preferred_element_type=jnp.float32)
        wide = wide.astype(jnp.bfloat16)
        at = pl.ds(pl.multiple_of(i * channels, channels), channels)
        for e in range(channels):
            held[at, e * cols : (e + 1) * cols] = wide[e * channels : (e + 1) * channels]

    total = channels * cols
    step = min(1024, total)
    out_left_ref[...] = jnp.zeros_like(out_left_ref)

    @pl.loop(0, total // step)
    def _(n):
        at = pl.ds(pl.multiple_of(n * step, step), step)
        part = held[:, at]
        sum_ref[:, at] += jnp.dot(left_ref[...], part, preferred_element_type=jnp.float32)
        out_left_ref[...] += lax.dot_general(
            right_ref[:, at], part, (((1,), (1,)), ((), ())), preferred_element_type=jnp.float32
        )

    out_left_ref[...] *= inverse


def contract(proj, grad, left, right, before, chunk, chunks):
    tile_rows, width, cols = grad.shape
    sequences = left.shape[0]
    rows = tile_rows // chunks
    channels = left.shape[1] // rows
    block = min(BLOCK_ROWS, rows)
    steps = rows // block
    flops = 2 * rows * cols * channels * channels * (width + 2 * sequences)
    whole = lambda shape: pl.BlockSpec(shape, lambda n: (0, 0))
    return pl.pallas_call(
        functools.partial(contract_block, channels, cols, 1.0 / sequences),
        grid=(steps,),
        in_specs=[
            whole(proj.shape),
            pl.BlockSpec((block, width, cols), lambda n: (chunk * steps + n, 0, 0)),
            pl.BlockSpec((sequences, block * channels), lambda n: (0, n)),
            whole(right.shape),
            whole(before.shape),
        ],
        out_specs=[
            pl.BlockSpec((sequences, block * channels), lambda n: (0, n)),
            whole(before.shape),
        ],
        out_shape=[
            jax.ShapeDtypeStruct((sequences, rows * channels), jnp.float32),
            jax.ShapeDtypeStruct(before.shape, jnp.float32),
        ],
        scratch_shapes=[pltpu.VMEM((block * channels, channels * cols), jnp.bfloat16)],
        input_output_aliases={4: 1},
        compiler_params=pltpu.CompilerParams(
            dimension_semantics=("arbitrary",), vmem_limit_bytes=56 * 1024 * 1024
        ),
        cost_estimate=pl.CostEstimate(
            flops=flops, bytes_accessed=rows * width * cols * 2 + before.size * 8, transcendentals=0
        ),
    )(proj, grad, left, right, before)


def gathered(proj, grad, left_own, right_own_flat):
    sequences_of = functools.partial(lax.all_gather, axis=0, tiled=True)
    right = sequences_of(right_own_flat, "row")
    per = left_own.shape[1] // CHUNKS
    lefts = [sequences_of(left_own[:, n * per : (n + 1) * per], "col") for n in range(CHUNKS)]
    summed = jnp.zeros(right.shape, jnp.float32)
    pieces = []
    for n in range(CHUNKS):
        part, summed = contract(proj, grad, lefts[n], right, summed, n, CHUNKS)
        pieces.append(lax.psum_scatter(part, "col", scatter_dimension=0, tiled=True))
    right_grad = lax.psum_scatter(summed, "row", scatter_dimension=0, tiled=True)
    return jnp.concatenate(pieces, axis=1), right_grad * (1.0 / right.shape[0])


def on_device(n_row, n_col, left_factor, right_factor, pair_grad, projection):
    tile_rows, width, cols = pair_grad.shape
    own, channels, _ = left_factor.shape
    right_own = right_factor.shape[0]
    proj = projection.reshape(channels, channels, width).transpose(1, 0, 2).reshape(channels * channels, width)
    right = right_factor.reshape(right_own, channels * cols)
    left = jnp.transpose(left_factor, (0, 2, 1)).reshape(own, tile_rows * channels)
    if own % 16 == 0 and right_own % 16 == 0 and cols % 256 == 0 and tile_rows % (4 * FUSED_ROWS) == 0:
        left_grad, right_grad = fused(proj, pair_grad, left, right, n_row, n_col)
    else:
        left_grad, right_grad = gathered(proj, pair_grad, left, right)
    left_grad = jnp.transpose(left_grad.reshape(own, tile_rows, channels), (0, 2, 1))
    return left_grad, right_grad.reshape(right_own, channels, cols)


def solution(mesh):
    placed = (P("col", None, "row"), P("row", None, "col"), P("row", None, "col"), P())
    return jax.shard_map(
        functools.partial(on_device, mesh.shape["row"], mesh.shape["col"]),
        mesh=mesh,
        in_specs=placed,
        out_specs=(P("col", None, "row"), P("row", None, "col")),
        check_vma=False,
    )
```

```python
import functools

import jax
import jax.numpy as jnp
from jax import lax
from jax.experimental import pallas as pl
from jax.experimental.pallas import tpu as pltpu
from jax.sharding import PartitionSpec as P

CHUNKS = 4
BLOCK_ROWS = 16
PASSES = 2
FUSED_ROWS = 32
STEP = 1024
AHEAD = 2
LANES = 128
MESH = pl.DeviceIdType.MESH
BF16 = jnp.bfloat16
F32 = jnp.float32


def fused_block(
    n_row, n_col, channels, proj_ref, grad_ref, left_ref, right_ref, out_left_ref, out_right_ref,
    held_0, held_1, proj, proj_wide, left_raw, right_raw, left_final, grads, lefts, rights, right_sum, left_sum, left_out, left_in, right_out, right_in, left_done,
    right_done, grad_sem, out_sem, own_sem, left_send, left_recv, right_send, right_recv, part_send, part_recv, sum_send, sum_recv,
):
    folds, _, width, cols = grad_ref.shape
    tile_rows = folds * LANES
    own, right_own = left_ref.shape[0] // channels, right_ref.shape[0] // channels
    sequences = own * n_col
    inverse = 1.0 / sequences
    rows = FUSED_ROWS
    blocks = tile_rows // rows
    chunks = blocks // 2
    pairs = PASSES * chunks
    some = channels // PASSES
    high = some * channels
    wide = some * cols
    deep = rows * channels
    span = 2 * deep
    step = min(STEP, wide)
    row, col = lax.axis_index("row"), lax.axis_index("col")

    def to_col(d):
        return {"col": lax.rem(col + d, n_col)}

    def to_row(d):
        return {"row": lax.rem(row + d, n_row)}

    half_row, half_col = n_row // 2, n_col // 2
    row_mate = row + 1 - 2 * lax.rem(row, 2)
    col_mate = col + 1 - 2 * lax.rem(col, 2)
    steps = wide // step

    def left_move(n, to, owner, k):
        at = (pl.ds(pl.multiple_of(owner * own, own), own), pl.ds(pl.multiple_of(k * span, span), span))
        return pltpu.make_async_remote_copy(
            lefts.at[at], lefts.at[at], left_send.at[n, k], left_recv.at[n, k], device_id={"col": to}, device_id_type=MESH
        )

    def right_move(n, to, owner, h):
        at = (pl.ds(pl.multiple_of(owner * right_own, right_own), right_own), pl.ds(pl.multiple_of(h * wide, wide), wide))
        return pltpu.make_async_remote_copy(
            rights.at[at], rights.at[at], right_send.at[n, h], right_recv.at[n, h], device_id={"row": to}, device_id_type=MESH
        )

    def give(move, me, mate, half, k):
        for d in range(1, half):
            move(d - 1, lax.rem(me + 2 * d, 2 * half), me, k).start()
        move(half - 1, mate, me, k).start()

    def forward(move, me, mate, half, k):
        for d in range(1, half):
            owner = lax.rem(me + 2 * (half - d), 2 * half)
            move(d - 1, mate, owner, k).wait_recv()
            move(half - 1 + d, mate, owner, k).start()

    def arrive(move, me, mate, half, k):
        for d in range(half):
            owner = lax.rem(mate + 2 * (half - d), 2 * half)
            move(half - 1 + d, mate, owner, k).wait_recv()

    def give_left(k):
        give(left_move, col, col_mate, half_col, k)

    def give_right(h):
        give(right_move, row, row_mate, half_row, h)

    def forward_left(k):
        forward(left_move, col, col_mate, half_col, k)

    def forward_right(h):
        forward(right_move, row, row_mate, half_row, h)

    def arrive_left(k):
        arrive(left_move, col, col_mate, half_col, k)

    def arrive_right(h):
        arrive(right_move, row, row_mate, half_row, h)

    def part_copy(d, k):
        at = pl.ds(pl.multiple_of(k * deep, deep), deep)
        to = lax.rem(col + d, n_col)
        return pltpu.make_async_remote_copy(
            left_out.at[pl.ds(pl.multiple_of(to * own, own), own), at], left_in.at[d - 1, :, at],
            part_send.at[d - 1, k], part_recv.at[d - 1, k], device_id=to_col(d), device_id_type=MESH,
        )

    def sum_copy(d, m):
        at = pl.ds(pl.multiple_of(m * step, step), step)
        to = lax.rem(row + d, n_row)
        return pltpu.make_async_remote_copy(
            right_out.at[pl.ds(pl.multiple_of(to * right_own, right_own), right_own), at], right_in.at[d - 1, :, at],
            sum_send.at[d - 1, m], sum_recv.at[d - 1, m], device_id=to_row(d), device_id_type=MESH,
        )

    def grad_copy(t, slot):
        high_rows = rows // folds
        at = pl.ds(lax.rem(t, blocks) * high_rows, high_rows)
        return pltpu.make_async_copy(grad_ref.at[:, at], grads.at[slot], grad_sem.at[slot])

    own_left = pltpu.make_async_copy(left_ref, left_raw, own_sem.at[0])
    own_right = pltpu.make_async_copy(right_ref, right_raw, own_sem.at[1])
    left_rows = pl.ds(pl.multiple_of(col * own, own), own)
    right_rows = pl.ds(pl.multiple_of(row * right_own, right_own), right_own)

    barrier = pltpu.get_barrier_semaphore()

    @pl.loop(1, n_col)
    def _(d):
        pl.semaphore_signal(barrier, inc=1, device_id=to_col(d), device_id_type=MESH)

    @pl.loop(1, n_row)
    def _(d):
        pl.semaphore_signal(barrier, inc=1, device_id=to_row(d), device_id_type=MESH)

    own_right.start()
    own_left.start()
    grad_copy(0, 0).start()
    grad_copy(1, 1).start()
    own_right.wait()
    halves = cols // LANES
    for u in range(halves):
        right_done[u] = right_raw[:, u * LANES : (u + 1) * LANES].astype(F32)
        for e in range(channels):
            at = e * cols + u * LANES
            rights[right_rows, at : at + LANES] = right_done[u, pl.ds(e, right_own, stride=channels), :].astype(BF16)
    own_left.wait()

    @pl.loop(0, own)
    def _(s):
        at = pl.ds(pl.multiple_of(s * channels, channels), channels)
        square = jnp.concatenate([left_raw[at, r * LANES : (r + 1) * LANES] for r in range(folds)], axis=0)
        left_done[pl.ds(pl.multiple_of(s * LANES, LANES), LANES), :] = square.astype(F32).T

    @pl.loop(0, LANES // 8)
    def _(m):
        for u in range(8):
            q = m * 8 + u
            at = pl.ds(pl.multiple_of(q * LANES, LANES), LANES)
            lefts[left_rows, at] = left_done[pl.ds(q, own, stride=LANES), :].astype(BF16)

    pl.semaphore_wait(barrier, n_col + n_row - 2)

    give_right(0)
    give_left(0)

    proj_wide[...] = proj_ref[...].astype(F32)
    for e in range(channels):
        proj[e * channels : (e + 1) * channels, :] = proj_wide[pl.ds(e, channels, stride=channels), :].astype(BF16)
    right_sum[...] = jnp.zeros_like(right_sum)
    left_sum[...] = jnp.zeros_like(left_sum)

    def produce_rows(first, count, h, slot, held):
        rows_of = pl.ds(pl.multiple_of(h * high, high), high)
        for r in range(count * folds):
            i = first * folds + r
            out = jnp.dot(
                proj[rows_of, :], grads[slot, r % folds, first + r // folds], preferred_element_type=F32
            ).astype(BF16)
            at = pl.ds(pl.multiple_of(i * channels, channels), channels)
            for e in range(some):
                held[at, e * cols : (e + 1) * cols] = out[e * channels : (e + 1) * channels]

    def consume_step(n, h, b, held):
        inside = pl.ds(pl.multiple_of(n * step, step), step)
        outside = pl.ds(pl.multiple_of(h * wide + n * step, step), step)
        deep_at = pl.ds(pl.multiple_of(b * deep, deep), deep)
        part = held[:, inside]
        right_sum[:, outside] += jnp.dot(lefts[:, deep_at], part, preferred_element_type=F32)
        left_sum[deep_at, :] += lax.dot_general(
            part, rights[:, outside], (((1,), (1,)), ((), ())), preferred_element_type=F32
        )

    def both(ahead, slot, into, h, b, held):
        @pl.loop(0, 1)
        def _(n):
            produce_rows(0, rows // folds, ahead, slot, into)
            for q in range(wide // step):
                consume_step(n + q, h, b, held)

    def send_left(k):
        piece = min(512, deep)

        @pl.loop(0, deep // piece)
        def _(q):
            at = pl.ds(pl.multiple_of(k * deep + q * piece, piece), piece)
            left_out[:, at] = left_sum[at, :].astype(BF16).T

        @pl.loop(1, n_col)
        def _(d):
            part_copy(d, k).start()

    def send_right(m):
        at = pl.ds(pl.multiple_of(m * step, step), step)
        right_out[:, at] = right_sum[:, at].astype(BF16)

        @pl.loop(1, n_row)
        def _(d):
            sum_copy(d, m).start()

    def total_left(k):
        @pl.loop(1, n_col)
        def _(d):
            part_copy(d, k).wait_recv()

        piece = min(512, deep)

        @pl.loop(0, deep // piece)
        def _(q):
            at = pl.ds(pl.multiple_of(k * deep + q * piece, piece), piece)
            total = left_out[left_rows, at].astype(F32)
            for d in range(n_col - 1):
                total += left_in[d, :, at].astype(F32)
            total *= inverse
            for u in range(piece // LANES):
                base = (k * deep + q * piece) // LANES + u
                left_done[pl.ds(base, own, stride=LANES), :] = total[:, u * LANES : (u + 1) * LANES]

    def total_right(h):
        @pl.loop(0, steps)
        def _(n):
            @pl.loop(1, n_row)
            def _(d):
                sum_copy(d, h * steps + n).wait_recv()

        @pl.loop(0, some)
        def _(n):
            e = h * some + n
            at = pl.ds(pl.multiple_of(e * cols, cols), cols)
            total = right_sum[right_rows, at]
            for d in range(n_row - 1):
                total += right_in[d, :, at].astype(F32)
            total *= inverse
            for u in range(halves):
                right_done[u, pl.ds(e, right_own, stride=channels), :] = total[:, u * LANES : (u + 1) * LANES]

    grad_copy(0, 0).wait()

    @pl.loop(0, rows // folds)
    def _(n):
        produce_rows(n, 1, 0, 0, held_0)

    forward_left(0)
    forward_right(0)
    give_left(1)
    arrive_right(0)

    def first_half(p):
        h, b = p // chunks, lax.rem(p, chunks) * 2

        @pl.when(p < chunks)
        def _():
            arrive_left(p)

        @pl.when(p < chunks - AHEAD)
        def _():
            give_left(p + AHEAD)

        @pl.when(p == 1)
        def _():
            give_right(1)

        @pl.when(p == 2)
        def _():
            forward_right(1)

        @pl.when(p == chunks)
        def _():
            arrive_right(1)

        grad_copy(2 * p + 1, 1).wait()

        @pl.when(p < pairs - 1)
        def _():
            grad_copy(2 * p + 2, 0).start()

        both(h, 1, held_1, h, b, held_0)

        @pl.when(p < chunks - 1)
        def _():
            forward_left(p + 1)

        @pl.when(p >= chunks)
        def _():
            send_left(b)

    @pl.loop(0, pairs - 1)
    def _(p):
        first_half(p)
        h, b = p // chunks, lax.rem(p, chunks) * 2 + 1
        ahead = (p + 1) // chunks
        grad_copy(2 * p + 2, 0).wait()
        grad_copy(2 * p + 3, 1).start()

        both(ahead, 0, held_0, h, b, held_1)

        @pl.when(p == chunks - 1)
        def _():
            @pl.loop(0, steps)
            def _(n):
                send_right(n)

        @pl.when(p >= chunks)
        def _():
            send_left(b)

    first_half(pairs - 1)

    @pl.loop(0, steps)
    def _(n):
        consume_step(n, PASSES - 1, blocks - 1, held_1)
        send_right((PASSES - 1) * steps + n)

    send_left(blocks - 1)
    total_right(0)

    @pl.loop(0, blocks)
    def _(k):
        total_left(k)

    @pl.loop(0, own)
    def _(s):
        square = left_done[pl.ds(pl.multiple_of(s * LANES, LANES), LANES), :].T
        at = pl.ds(pl.multiple_of(s * channels, channels), channels)
        for r in range(folds):
            left_final[at, r * LANES : (r + 1) * LANES] = square[r * channels : (r + 1) * channels]

    left_copy_out = pltpu.make_async_copy(left_final, out_left_ref, own_sem.at[0])
    left_copy_out.start()
    total_right(1)
    right_copies_out = [
        pltpu.make_async_copy(right_done.at[u], out_right_ref.at[:, u * LANES : (u + 1) * LANES], out_sem.at[u])
        for u in range(halves)
    ]
    for copy in right_copies_out:
        copy.start()

    @pl.loop(0, chunks)
    def _(k):
        @pl.loop(0, n_col - 1)
        def _(n):
            left_move(n, col_mate, col, k).wait_send()

    @pl.loop(0, blocks)
    def _(k):
        @pl.loop(1, n_col)
        def _(d):
            part_copy(d, k).wait_send()

    @pl.loop(0, PASSES)
    def _(h):
        @pl.loop(0, n_row - 1)
        def _(n):
            right_move(n, row_mate, row, h).wait_send()

    @pl.loop(0, PASSES * steps)
    def _(m):
        @pl.loop(1, n_row)
        def _(d):
            sum_copy(d, m).wait_send()

    left_copy_out.wait()
    for copy in right_copies_out:
        copy.wait()


def fused(proj, grad, left, right, n_row, n_col):
    tile_rows, width, cols = grad.shape
    own, channels, _ = left.shape
    right_own = right.shape[0]
    folds = tile_rows // LANES
    grad = grad.reshape(folds, LANES, width, cols)
    left = left.reshape(own * channels, tile_rows)
    right = right.reshape(right_own * channels, cols)
    sequences = own * n_col
    rows = FUSED_ROWS
    chunks = tile_rows // rows // 2
    wide = channels // PASSES * cols
    steps = wide // min(STEP, wide)
    flops = 2 * tile_rows * cols * channels * channels * (width + 2 * sequences)
    anywhere = pl.BlockSpec(memory_space=pl.ANY)
    held = pltpu.VMEM((rows * channels, channels // PASSES * cols), BF16)
    dma = pltpu.SemaphoreType.DMA
    return pl.pallas_call(
        functools.partial(fused_block, n_row, n_col, channels),
        in_specs=[pl.BlockSpec(memory_space=pltpu.VMEM), anywhere, anywhere, anywhere],
        out_specs=[anywhere, anywhere],
        out_shape=[jax.ShapeDtypeStruct(left.shape, F32), jax.ShapeDtypeStruct(right.shape, F32)],
        scratch_shapes=[
            held,
            held,
            pltpu.VMEM(proj.shape, BF16),
            pltpu.VMEM(proj.shape, F32),
            pltpu.VMEM(left.shape, BF16),
            pltpu.VMEM(right.shape, BF16),
            pltpu.VMEM(left.shape, F32),
            pltpu.VMEM((2, folds, rows // folds, width, cols), BF16),
            pltpu.VMEM((sequences, tile_rows * channels), BF16),
            pltpu.VMEM((sequences, channels * cols), BF16),
            pltpu.VMEM((sequences, channels * cols), F32),
            pltpu.VMEM((tile_rows * channels, sequences), F32),
            pltpu.VMEM((sequences, tile_rows * channels), BF16),
            pltpu.VMEM((n_col - 1, own, tile_rows * channels), BF16),
            pltpu.VMEM((sequences, channels * cols), BF16),
            pltpu.VMEM((n_row - 1, right_own, channels * cols), BF16),
            pltpu.VMEM((own * LANES, folds * channels), F32),
            pltpu.VMEM((cols // LANES, right_own * channels, LANES), F32),
            dma((2,)),
            dma((cols // LANES,)),
            dma((2,)),
            dma((n_col - 1, chunks)),
            dma((n_col - 1, chunks)),
            dma((n_row - 1, PASSES)),
            dma((n_row - 1, PASSES)),
            dma((n_col - 1, 2 * chunks)),
            dma((n_col - 1, 2 * chunks)),
            dma((n_row - 1, PASSES * steps)),
            dma((n_row - 1, PASSES * steps)),
        ],
        compiler_params=pltpu.CompilerParams(
            collective_id=0, has_side_effects=True, vmem_limit_bytes=62 * 1024 * 1024
        ),
        cost_estimate=pl.CostEstimate(flops=flops, bytes_accessed=2 * grad.size * 2, transcendentals=0),
    )(proj, grad, left, right)


def contract_block(channels, cols, inverse, proj_ref, grad_ref, left_ref, right_ref, before_ref, out_left_ref, sum_ref, held):
    rows = grad_ref.shape[0]

    @pl.when(pl.program_id(0) == 0)
    def _():
        sum_ref[...] = before_ref[...]

    @pl.loop(0, rows)
    def _(i):
        wide = jnp.dot(proj_ref[...], grad_ref[i], preferred_element_type=jnp.float32)
        wide = wide.astype(jnp.bfloat16)
        at = pl.ds(pl.multiple_of(i * channels, channels), channels)
        for e in range(channels):
            held[at, e * cols : (e + 1) * cols] = wide[e * channels : (e + 1) * channels]

    total = channels * cols
    step = min(1024, total)
    out_left_ref[...] = jnp.zeros_like(out_left_ref)

    @pl.loop(0, total // step)
    def _(n):
        at = pl.ds(pl.multiple_of(n * step, step), step)
        part = held[:, at]
        sum_ref[:, at] += jnp.dot(left_ref[...], part, preferred_element_type=jnp.float32)
        out_left_ref[...] += lax.dot_general(
            right_ref[:, at], part, (((1,), (1,)), ((), ())), preferred_element_type=jnp.float32
        )

    out_left_ref[...] *= inverse


def contract(proj, grad, left, right, before, chunk, chunks):
    tile_rows, width, cols = grad.shape
    sequences = left.shape[0]
    rows = tile_rows // chunks
    channels = left.shape[1] // rows
    block = min(BLOCK_ROWS, rows)
    steps = rows // block
    flops = 2 * rows * cols * channels * channels * (width + 2 * sequences)
    whole = lambda shape: pl.BlockSpec(shape, lambda n: (0, 0))
    return pl.pallas_call(
        functools.partial(contract_block, channels, cols, 1.0 / sequences),
        grid=(steps,),
        in_specs=[
            whole(proj.shape),
            pl.BlockSpec((block, width, cols), lambda n: (chunk * steps + n, 0, 0)),
            pl.BlockSpec((sequences, block * channels), lambda n: (0, n)),
            whole(right.shape),
            whole(before.shape),
        ],
        out_specs=[
            pl.BlockSpec((sequences, block * channels), lambda n: (0, n)),
            whole(before.shape),
        ],
        out_shape=[
            jax.ShapeDtypeStruct((sequences, rows * channels), jnp.float32),
            jax.ShapeDtypeStruct(before.shape, jnp.float32),
        ],
        scratch_shapes=[pltpu.VMEM((block * channels, channels * cols), jnp.bfloat16)],
        input_output_aliases={4: 1},
        compiler_params=pltpu.CompilerParams(
            dimension_semantics=("arbitrary",), vmem_limit_bytes=56 * 1024 * 1024
        ),
        cost_estimate=pl.CostEstimate(
            flops=flops, bytes_accessed=rows * width * cols * 2 + before.size * 8, transcendentals=0
        ),
    )(proj, grad, left, right, before)


def gathered(proj, grad, left_own, right_own_flat):
    sequences_of = functools.partial(lax.all_gather, axis=0, tiled=True)
    right = sequences_of(right_own_flat, "row")
    per = left_own.shape[1] // CHUNKS
    lefts = [sequences_of(left_own[:, n * per : (n + 1) * per], "col") for n in range(CHUNKS)]
    summed = jnp.zeros(right.shape, jnp.float32)
    pieces = []
    for n in range(CHUNKS):
        part, summed = contract(proj, grad, lefts[n], right, summed, n, CHUNKS)
        pieces.append(lax.psum_scatter(part, "col", scatter_dimension=0, tiled=True))
    right_grad = lax.psum_scatter(summed, "row", scatter_dimension=0, tiled=True)
    return jnp.concatenate(pieces, axis=1), right_grad * (1.0 / right.shape[0])


def on_device(n_row, n_col, left_factor, right_factor, pair_grad, projection):
    tile_rows, width, cols = pair_grad.shape
    own, channels, _ = left_factor.shape
    right_own = right_factor.shape[0]
    folds = tile_rows // LANES
    fits = own % 16 == 0 and right_own % 16 == 0 and cols % 256 == 0 and tile_rows % LANES == 0
    fits = fits and n_row % 2 == 0 and n_col % 2 == 0 and tile_rows // FUSED_ROWS >= 8
    if fits and folds * channels == LANES and FUSED_ROWS % folds == 0:
        left_grad, right_grad = fused(projection, pair_grad, left_factor, right_factor, n_row, n_col)
        return left_grad.reshape(left_factor.shape), right_grad.reshape(right_factor.shape)
    proj = projection.reshape(channels, channels, width).transpose(1, 0, 2).reshape(channels * channels, width)
    right = right_factor.reshape(right_own, channels * cols)
    left = jnp.transpose(left_factor, (0, 2, 1)).reshape(own, tile_rows * channels)
    left_grad, right_grad = gathered(proj, pair_grad, left, right)
    left_grad = jnp.transpose(left_grad.reshape(own, tile_rows, channels), (0, 2, 1))
    return left_grad, right_grad.reshape(right_own, channels, cols)


def solution(mesh):
    placed = (P("col", None, "row"), P("row", None, "col"), P("row", None, "col"), P())
    return jax.shard_map(
        functools.partial(on_device, mesh.shape["row"], mesh.shape["col"]),
        mesh=mesh,
        in_specs=placed,
        out_specs=(P("col", None, "row"), P("row", None, "col")),
        check_vma=False,
    )
```
